32 devices in a mesh: freq: 2 (over x), row: 16 (over z, y, core).
Axes of the slice: x: 2, y: 2, z: 4, core: 2. Of those that a mesh axis runs over, the one named last changes fastest.
Arguments:
- data_real: bfloat16 [16384, 8192], P(('freq', 'row')), parts along dimension 0, may hold values from -6 to 6
- data_imag: bfloat16 [16384, 8192], P(('freq', 'row')), parts along dimension 0, may hold values from -6 to 6
- counts: int32 [8, 8], replicated, may hold values from 0 to 4
- source_cols: int32 [128], replicated, may hold values from 0 to 8191, as said below
Outputs:
- pred_real: float32 [16384, 128], P(('freq', 'row')), parts along dimension 0
- pred_imag: float32 [16384, 128], P(('freq', 'row')), parts along dimension 0
The draws below stay inside these ranges and needn't reach their ends.
There are 2 independent parts, one for each index of `freq`. The reference program is written for one: setup_inputs(seed, part) draws one part's arguments, and reference() takes and returns one part's arrays. A program takes and returns all parts, laid end to end along the dimension named above; an argument that names none is the same for every part. Nothing has to cross between parts.
Inputs may be any that keep to these rules, and one draw needn't show every extreme that they name: `source_cols`: 128 distinct grid points; 0 and 8191 are always among them.
All inputs are finite; a program needn't handle non-finite values.
Results may differ from the reference program's by a relative error of at most 0.0029.
Values may be sent and summed in bfloat16 or wider, within the bound.
A program may use at most 128 MiB of HBM per device.

```python
import jax
import jax.numpy as jnp
from jax import lax

N = 8192
SRC = 128
TILES = 8


def draw_source_cols(key, part):
    inner = jax.random.permutation(jax.random.fold_in(key, 11), N - 2)[:SRC - 2] + 1
    both = jnp.concatenate([jnp.array([0, N - 1], jnp.int32), inner.astype(jnp.int32)])
    order = jax.random.permutation(jax.random.fold_in(key, 12), SRC)
    return both[order]


def place_ends(values, rng, smallest, largest):
    shape = values.shape
    index_at = [jax.random.randint(jax.random.fold_in(rng, axis), (), 0, shape[axis]) for axis in range(len(shape))]
    values = values.at[tuple(index_at)].set(smallest)
    longest = shape.index(max(shape))
    index_at[longest] = (index_at[longest] + 1) % shape[longest]
    return values.at[tuple(index_at)].set(largest)


def strengthened(drawn, own_key, source, target, blocks, factor):
    def block_of(dim):
        return (jnp.arange(drawn.shape[dim]) // (drawn.shape[dim] // blocks)).reshape((-1,) + (1,) * (drawn.ndim - 1 - dim))

    one_side = jax.random.permutation(own_key, blocks)[block_of(target)]
    far = (block_of(target) + blocks // 2) % blocks
    return jnp.where((block_of(source) == one_side) | (block_of(source) == far), factor * drawn, drawn)


def level_of(own_key, dims, cuts, least, high):
    def one(position, shards_of):
        draws = jax.random.uniform(jax.random.fold_in(jax.random.fold_in(own_key, 6), position), (shards_of,), jnp.float32, least / len(cuts), high / len(cuts))
        return jnp.repeat(jnp.exp(draws), dims[position] // shards_of).reshape((-1,) + (1,) * (len(dims) - position - 1))

    factor_of = one(*cuts[0])
    for cut in cuts[1:]:
        factor_of = factor_of * one(*cut)
    return factor_of


def noise_with(key, shape, deviation, most, pieces, heavy, kind=jnp.bfloat16):
    entries = deviation * jax.random.normal(key, shape, jnp.float32)
    if pieces:
        entries = entries * level_of(key, shape, pieces, -0.22, 0.18)
    return jnp.clip(strengthened(entries, jax.random.fold_in(key, 3), *heavy), -most, most).astype(kind)


def setup_inputs(seed: int = 0, part: int = 0) -> dict:
    streams_of = jax.random.split(jax.random.key(seed), 5)
    part_keys = jax.random.split(jax.random.fold_in(streams_of[4], part), 5)
    data_real = noise_with(part_keys[0], (N, N), 1.0, 6.0, ((0, 16),), (0, 1, 16, 2.0))
    data_imag = noise_with(part_keys[1], (N, N), 1.0, 6.0, ((0, 16),), (0, 1, 16, 2.0))
    counts = place_ends(jax.random.randint(streams_of[2], (TILES, TILES), 0, 5), jax.random.fold_in(streams_of[2], 1), 0, 4).astype(jnp.int32)
    source_cols = draw_source_cols(jax.random.fold_in(streams_of[4], 71), part)
    return {"data_real": data_real, "data_imag": data_imag, "counts": counts, "source_cols": source_cols}


def symmetrize(data_real, data_imag, counts, row_ids):
    width = data_real.shape[1]
    tile = width // TILES
    table = counts.astype(jnp.float32)
    col_tiles = jnp.arange(width, dtype=jnp.int32) // tile
    row_tiles = row_ids // tile
    forward = table[row_tiles][:, col_tiles]
    backward = table.T[row_tiles][:, col_tiles]
    denom = jnp.maximum(forward + backward, 1.0)
    results = []
    for data in (data_real, data_imag):
        own = data[row_ids, :].astype(jnp.float32)
        mirror = data[:, row_ids].T.astype(jnp.float32)
        results.append(((forward * own + backward * mirror) / denom).astype(jnp.bfloat16))
    return (results[0], results[1])

def reference(data_real, data_imag, counts, source_cols):
    width = data_real.shape[0]
    tile = width // TILES
    src_real, src_imag = symmetrize(data_real, data_imag, counts, source_cols.astype(jnp.int32))
    panel_real = src_real.T
    panel_imag = src_imag.T
    factor = -1.0 / jnp.sqrt(jnp.float32(width))

    def block(index):
        row_ids = (index * tile + jnp.arange(tile, dtype=jnp.int32)).astype(jnp.int32)
        sym_real, sym_imag = symmetrize(data_real, data_imag, counts, row_ids)
        real = jnp.dot(sym_real, panel_real, preferred_element_type=jnp.float32) - jnp.dot(sym_imag, panel_imag, preferred_element_type=jnp.float32)
        imag = jnp.dot(sym_real, panel_imag, preferred_element_type=jnp.float32) + jnp.dot(sym_imag, panel_real, preferred_element_type=jnp.float32)
        return (factor * real, factor * imag)
    real, imag = lax.map(block, jnp.arange(TILES, dtype=jnp.int32))
    count = source_cols.shape[0]
    return (real.reshape(width, count), imag.reshape(width, count))
```

```python
import functools
import math

import jax
import jax.numpy as jnp
from jax import lax
from jax.experimental import pallas as pl
from jax.experimental.pallas import tpu as pltpu
from jax.sharding import PartitionSpec as P

TILES = 8
SEND = jnp.float32
NT = (((1,), (1,)), ((), ()))
NN = (((1,), (0,)), ((), ()))


def dot(a, b, dims=NN):
    return lax.dot_general(a, b, dims, preferred_element_type=jnp.float32)


def pick_kernel(row0_ref, cols_ref, dr_ref, di_ref, rows_ref, own_ref):
    j = pl.program_id(0)
    height, width = dr_ref.shape
    cols = cols_ref[...]
    sources = cols.shape[0]
    at_row = row0_ref[0] + lax.broadcasted_iota(jnp.int32, (sources, height), 1)
    pick_rows = (cols == at_row).astype(jnp.float32).astype(jnp.bfloat16)
    at_col = j * width + lax.broadcasted_iota(jnp.int32, (sources, width), 1)
    pick_cols = (cols == at_col).astype(jnp.float32).astype(jnp.bfloat16)
    dr = dr_ref[...]
    di = di_ref[...]
    rows_ref[0, :sources, :] = dot(pick_rows, dr).astype(jnp.bfloat16)
    rows_ref[0, sources:, :] = dot(pick_rows, di).astype(jnp.bfloat16)

    @pl.when(j == 0)
    def _():
        own_ref[...] = jnp.zeros_like(own_ref)

    own_ref[:sources, :] += dot(pick_cols, dr, NT)
    own_ref[sources:, :] += dot(pick_cols, di, NT)


def turned(panel):
    half = panel.shape[0] // 2
    return jnp.concatenate([-panel[half:], panel[:half]], axis=0)


def back_kernel(scale_ref, panel_ref, dr_ref, di_ref, out_ref):
    j = pl.program_id(0)
    panel = panel_ref[...]
    total = dot(panel, dr_ref[...]) + dot(turned(panel), di_ref[...])
    out_ref[0] = (scale_ref[j] * total).astype(out_ref.dtype)


def front_kernel(scale_ref, panels_ref, back_ref, dr_ref, di_ref, real_ref, imag_ref, acc, *, factor):
    j = pl.program_id(0)

    @pl.when(j == 0)
    def _():
        acc[...] = jnp.zeros_like(acc)

    panel = panels_ref[0]
    acc[...] += scale_ref[j] * (dot(dr_ref[...], panel, NT) + dot(di_ref[...], turned(panel), NT))

    @pl.when(j == pl.num_programs(0) - 1)
    def _():
        total = factor * (acc[...] + back_ref[0].astype(jnp.float32).T)
        half = total.shape[1] // 2
        real_ref[...] = total[:, :half]
        imag_ref[...] = total[:, half:]


def shards(n, data_real, data_imag, counts, source_cols):
    rows, width = data_real.shape
    sources = source_cols.shape[0]
    tile = width // TILES
    factor = -1.0 / math.sqrt(width)
    me = lax.axis_index("row")
    row0 = me * rows
    table = counts.astype(jnp.float32)
    forward = lax.dynamic_index_in_dim(table, row0 // tile, 0, keepdims=False)
    backward = lax.dynamic_index_in_dim(table, row0 // tile, 1, keepdims=False)
    denom = jnp.maximum(forward + backward, 1.0)
    scale = jnp.repeat(forward / denom, n // TILES)
    smem = pl.BlockSpec(memory_space=pltpu.SMEM)
    whole = lambda shape: pl.BlockSpec(shape, lambda j: (0,) * len(shape))
    block = pl.BlockSpec((rows, rows), lambda j: (0, j))
    params = pltpu.CompilerParams(vmem_limit_bytes=48 << 20)
    picked, own = pl.pallas_call(
        pick_kernel,
        grid=(n,),
        out_shape=(
            jax.ShapeDtypeStruct((n, 2 * sources, rows), jnp.bfloat16),
            jax.ShapeDtypeStruct((2 * sources, rows), jnp.float32),
        ),
        in_specs=[smem, whole((sources, 1)), block, block],
        out_specs=(
            pl.BlockSpec((1, 2 * sources, rows), lambda j: (j, 0, 0)),
            whole((2 * sources, rows)),
        ),
        compiler_params=params,
    )(row0.reshape(1), source_cols.reshape(sources, 1), data_real, data_imag)
    mirror = lax.psum_scatter(picked, "row", scatter_dimension=0, tiled=True)[0]
    tiles = source_cols // tile
    w = jnp.tile(forward[tiles], 2)[:, None]
    v = jnp.tile(backward[tiles], 2)[:, None]
    panel = ((w * own + v * mirror.astype(jnp.float32)) / jnp.maximum(w + v, 1.0)).astype(jnp.bfloat16)
    panels = lax.all_gather(panel, "row", axis=0, tiled=False)
    back = pl.pallas_call(
        back_kernel,
        grid=(n,),
        out_shape=jax.ShapeDtypeStruct((n, 2 * sources, rows), SEND),
        in_specs=[smem, whole((2 * sources, rows)), block, block],
        out_specs=pl.BlockSpec((1, 2 * sources, rows), lambda j: (j, 0, 0)),
        compiler_params=params,
    )(scale, panel, data_real, data_imag)
    back = lax.psum_scatter(back, "row", scatter_dimension=0, tiled=True)
    return pl.pallas_call(
        functools.partial(front_kernel, factor=factor),
        grid=(n,),
        out_shape=(jax.ShapeDtypeStruct((rows, sources), jnp.float32),) * 2,
        in_specs=[
            smem,
            pl.BlockSpec((1, 2 * sources, rows), lambda j: (j, 0, 0)),
            whole((1, 2 * sources, rows)),
            block,
            block,
        ],
        out_specs=(whole((rows, sources)),) * 2,
        scratch_shapes=[pltpu.VMEM((rows, 2 * sources), jnp.float32)],
        compiler_params=params,
    )(scale, panels, back, data_real, data_imag)


def generic(data_real, data_imag, counts, source_cols):
    rows, width = data_real.shape
    sources = source_cols.shape[0]
    tile = width // TILES
    factor = -1.0 / math.sqrt(width)
    row0 = lax.axis_index("row") * rows
    table = counts.astype(jnp.float32)
    forward = lax.dynamic_index_in_dim(table, row0 // tile, 0, keepdims=False)
    backward = lax.dynamic_index_in_dim(table, row0 // tile, 1, keepdims=False)
    scale = jnp.repeat(forward / jnp.maximum(forward + backward, 1.0), tile)
    at_row = row0 + jnp.arange(rows, dtype=jnp.int32)
    pick_rows = (source_cols[:, None] == at_row[None, :]).astype(jnp.bfloat16)
    tn = (((0,), (1,)), ((), ()))
    picked = jnp.concatenate([dot(data_real, pick_rows, tn), dot(data_imag, pick_rows, tn)], axis=1)
    mirror = lax.psum_scatter(picked.astype(jnp.bfloat16), "row", scatter_dimension=0, tiled=True)
    own = jnp.concatenate([jnp.take(data_real, source_cols, axis=1), jnp.take(data_imag, source_cols, axis=1)], axis=1)
    tiles = source_cols // tile
    w = jnp.tile(forward[tiles], 2)[None, :]
    v = jnp.tile(backward[tiles], 2)[None, :]
    panel = (w * own.astype(jnp.float32) + v * mirror.astype(jnp.float32)) / jnp.maximum(w + v, 1.0)
    panel = panel.astype(jnp.bfloat16)
    swap = lambda p: jnp.concatenate([-p[:, sources:], p[:, :sources]], axis=1)
    panels = lax.all_gather(panel, "row", axis=0, tiled=True)
    tt = (((0,), (0,)), ((), ()))
    back = scale[:, None] * (dot(data_real, panel, tt) + dot(data_imag, swap(panel), tt))
    back = lax.psum_scatter(back, "row", scatter_dimension=0, tiled=True)
    steps = jnp.stack([
        s * (
            dot(data_real[:, t * tile : (t + 1) * tile], panels[t * tile : (t + 1) * tile])
            + dot(data_imag[:, t * tile : (t + 1) * tile], swap(panels[t * tile : (t + 1) * tile]))
        )
        for t, s in enumerate(scale[::tile])
    ])
    total = factor * (steps.sum(0) + back)
    return total[:, :sources], total[:, sources:]


def solution(mesh):
    n = mesh.shape["row"]

    def body(data_real, data_imag, counts, source_cols):
        rows = data_real.shape[0]
        if rows % 128 == 0 and n % TILES == 0:
            return shards(n, data_real, data_imag, counts, source_cols)
        return generic(data_real, data_imag, counts, source_cols)

    placed = (P(("freq", "row"), None), P(("freq", "row"), None), P(), P())
    return jax.shard_map(
        body,
        mesh=mesh,
        in_specs=placed,
        out_specs=(P(("freq", "row"), None), P(("freq", "row"), None)),
        check_vma=False,
    )
```

```python
import functools
import math

import jax
import jax.numpy as jnp
from jax import lax
from jax.experimental import pallas as pl
from jax.experimental.pallas import tpu as pltpu
from jax.sharding import PartitionSpec as P

TILES = 8
NT = (((1,), (1,)), ((), ()))
NN = (((1,), (0,)), ((), ()))


def dot(a, b, dims=NN):
    return lax.dot_general(a, b, dims, preferred_element_type=jnp.float32)


def pick_kernel(info_ref, cols_ref, dr_ref, di_ref, rows_ref, own_ref):
    k = pl.program_id(0)
    height, width = dr_ref.shape
    cols = cols_ref[...]
    sources = cols.shape[0]
    at_row = info_ref[1] + lax.broadcasted_iota(jnp.int32, (sources, height), 1)
    pick_rows = (cols == at_row).astype(jnp.float32).astype(jnp.bfloat16)
    at_col = (2 * k + info_ref[0]) * width + lax.broadcasted_iota(jnp.int32, (sources, width), 1)
    pick_cols = (cols == at_col).astype(jnp.float32).astype(jnp.bfloat16)
    dr = dr_ref[...]
    di = di_ref[...]
    rows_ref[0, :sources, :] = dot(pick_rows, dr).astype(jnp.bfloat16)
    rows_ref[0, sources:, :] = dot(pick_rows, di).astype(jnp.bfloat16)

    @pl.when(k == 0)
    def _():
        own_ref[...] = jnp.zeros_like(own_ref)

    own_ref[:sources, :] += dot(pick_cols, dr, NT)
    own_ref[sources:, :] += dot(pick_cols, di, NT)


def turned(panel):
    half = panel.shape[0] // 2
    return jnp.concatenate([-panel[half:], panel[:half]], axis=0)


def back_kernel(info_ref, scale_ref, panel_ref, dr_ref, di_ref, out_ref):
    j = 2 * pl.program_id(0) + info_ref[0]
    panel = panel_ref[...]
    total = dot(panel, dr_ref[...]) + dot(turned(panel), di_ref[...])
    out_ref[0] = (scale_ref[j] * total).astype(out_ref.dtype)


def front_kernel(scale_ref, panels_ref, dr_ref, di_ref, out_ref):
    j = pl.program_id(0)

    @pl.when(j == 0)
    def _():
        out_ref[...] = jnp.zeros_like(out_ref)

    panel = panels_ref[0]
    out_ref[...] += scale_ref[j] * (dot(dr_ref[...], panel, NT) + dot(di_ref[...], turned(panel), NT))


def final_kernel(front_ref, first_ref, second_ref, real_ref, imag_ref, *, factor):
    sources = first_ref.shape[0]
    real_ref[...] = factor * (front_ref[:, :sources] + first_ref[...].T)
    imag_ref[...] = factor * (front_ref[:, sources:] + second_ref[...].T)


def swap(x, bit):
    n = lax.axis_size("row")
    return lax.ppermute(x, "row", [(i, i ^ (1 << bit)) for i in range(n)])


def halved(x, me, bit, axis):
    mine = (me >> bit) & 1
    got = swap(lax.dynamic_index_in_dim(x, 1 - mine, axis, False).astype(jnp.bfloat16), bit)
    return lax.dynamic_index_in_dim(x, mine, axis, False) + got.astype(x.dtype)


def scattered(kept, got, me):
    half = kept.shape[1] // 2
    total = kept + got.astype(kept.dtype)
    first = total[:, :half].reshape((2, 2, 2) + (half, kept.shape[2]))
    second = total[:, half:].reshape((2, 2, 2) + (half, kept.shape[2]))
    first = halved(first, me, 1, 2)
    second = halved(second, me, 2, 1)
    first = halved(first, me, 2, 1)
    second = halved(second, me, 3, 0)
    first = halved(first, me, 3, 0)
    second = halved(second, me, 1, 0)
    return first, second


def shards(n, data_real, data_imag, counts, source_cols):
    rows, width = data_real.shape
    sources = source_cols.shape[0]
    pair = 2 * sources
    tile = width // TILES
    factor = -1.0 / math.sqrt(width)
    me = lax.axis_index("row")
    core = me & 1
    row0 = me * rows
    table = counts.astype(jnp.float32)
    forward = lax.dynamic_index_in_dim(table, row0 // tile, 0, keepdims=False)
    backward = lax.dynamic_index_in_dim(table, row0 // tile, 1, keepdims=False)
    denom = jnp.maximum(forward + backward, 1.0)
    scale = jnp.repeat(forward / denom, n // TILES)
    smem = pl.BlockSpec(memory_space=pltpu.SMEM)
    params = pltpu.CompilerParams(vmem_limit_bytes=32 << 20)
    cost = pl.CostEstimate(flops=2 * rows * width * pair, bytes_accessed=4 * rows * width, transcendentals=0)
    half_cost = pl.CostEstimate(flops=rows * width * pair, bytes_accessed=2 * rows * width, transcendentals=0)
    whole = lambda shape: pl.BlockSpec(shape, lambda j, *refs: (0,) * len(shape))
    strided = pl.BlockSpec((rows, rows), lambda k, info: (0, 2 * k + info[0]))
    stacked = pl.BlockSpec((1, pair, rows), lambda k, *refs: (k, 0, 0))
    cols = source_cols.reshape(sources, 1)

    def pick(target):
        return pl.pallas_call(
            pick_kernel,
            grid_spec=pltpu.PrefetchScalarGridSpec(
                num_scalar_prefetch=1,
                grid=(n // 2,),
                in_specs=[whole((sources, 1)), strided, strided],
                out_specs=(stacked, whole((pair, rows))),
            ),
            out_shape=(
                jax.ShapeDtypeStruct((n // 2, pair, rows), jnp.bfloat16),
                jax.ShapeDtypeStruct((pair, rows), jnp.float32),
            ),
            compiler_params=params,
            cost_estimate=half_cost,
        )(jnp.stack([target, row0]), cols, data_real, data_imag)

    def back(target, kind, panel):
        return pl.pallas_call(
            back_kernel,
            grid_spec=pltpu.PrefetchScalarGridSpec(
                num_scalar_prefetch=1,
                grid=(n // 2,),
                in_specs=[smem, whole((pair, rows)), strided, strided],
                out_specs=stacked,
            ),
            out_shape=jax.ShapeDtypeStruct((n // 2, pair, rows), kind),
            compiler_params=params,
            cost_estimate=half_cost,
        )(target.reshape(1), scale, panel, data_real, data_imag)

    sent, own_a = pick(1 - core)
    got = swap(sent, 0)
    kept, own_b = pick(core)
    own = own_a + own_b
    tiles = (source_cols // tile)[:, None] == jnp.arange(TILES, dtype=jnp.int32)[None, :]
    w = jnp.tile(jnp.sum(jnp.where(tiles, forward, 0.0), axis=1), 2)[:, None]
    v = jnp.tile(jnp.sum(jnp.where(tiles, backward, 0.0), axis=1), 2)[:, None]
    mirror = jnp.concatenate(scattered(kept, got, me), axis=0).astype(jnp.float32)
    panel = ((w * own + v * mirror) / jnp.maximum(w + v, 1.0)).astype(jnp.bfloat16)
    panels = lax.all_gather(panel, "row", axis=0, tiled=False)
    sent = back(1 - core, jnp.bfloat16, panel)
    got = swap(sent, 0)
    kept = back(core, jnp.float32, panel)
    first, second = scattered(kept, got, me)
    front = pl.pallas_call(
        front_kernel,
        grid=(n,),
        out_shape=jax.ShapeDtypeStruct((rows, pair), jnp.float32),
        in_specs=[
            smem,
            stacked,
            pl.BlockSpec((rows, rows), lambda j: (0, j)),
            pl.BlockSpec((rows, rows), lambda j: (0, j)),
        ],
        out_specs=whole((rows, pair)),
        compiler_params=params,
        cost_estimate=cost,
    )(scale, panels, data_real, data_imag)
    return pl.pallas_call(
        functools.partial(final_kernel, factor=factor),
        out_shape=(jax.ShapeDtypeStruct((rows, sources), jnp.float32),) * 2,
        compiler_params=params,
    )(front, first, second)


def generic(data_real, data_imag, counts, source_cols):
    rows, width = data_real.shape
    sources = source_cols.shape[0]
    tile = width // TILES
    factor = -1.0 / math.sqrt(width)
    row0 = lax.axis_index("row") * rows
    table = counts.astype(jnp.float32)
    forward = lax.dynamic_index_in_dim(table, row0 // tile, 0, keepdims=False)
    backward = lax.dynamic_index_in_dim(table, row0 // tile, 1, keepdims=False)
    scale = jnp.repeat(forward / jnp.maximum(forward + backward, 1.0), tile)
    at_row = row0 + jnp.arange(rows, dtype=jnp.int32)
    pick_rows = (source_cols[:, None] == at_row[None, :]).astype(jnp.bfloat16)
    tn = (((0,), (1,)), ((), ()))
    picked = jnp.concatenate([dot(data_real, pick_rows, tn), dot(data_imag, pick_rows, tn)], axis=1)
    mirror = lax.psum_scatter(picked.astype(jnp.bfloat16), "row", scatter_dimension=0, tiled=True)
    own = jnp.concatenate([jnp.take(data_real, source_cols, axis=1), jnp.take(data_imag, source_cols, axis=1)], axis=1)
    tiles = source_cols // tile
    w = jnp.tile(forward[tiles], 2)[None, :]
    v = jnp.tile(backward[tiles], 2)[None, :]
    panel = (w * own.astype(jnp.float32) + v * mirror.astype(jnp.float32)) / jnp.maximum(w + v, 1.0)
    panel = panel.astype(jnp.bfloat16)
    swap = lambda p: jnp.concatenate([-p[:, sources:], p[:, :sources]], axis=1)
    panels = lax.all_gather(panel, "row", axis=0, tiled=True)
    tt = (((0,), (0,)), ((), ()))
    back = scale[:, None] * (dot(data_real, panel, tt) + dot(data_imag, swap(panel), tt))
    back = lax.psum_scatter(back, "row", scatter_dimension=0, tiled=True)
    steps = jnp.stack([
        s * (
            dot(data_real[:, t * tile : (t + 1) * tile], panels[t * tile : (t + 1) * tile])
            + dot(data_imag[:, t * tile : (t + 1) * tile], swap(panels[t * tile : (t + 1) * tile]))
        )
        for t, s in enumerate(scale[::tile])
    ])
    total = factor * (steps.sum(0) + back)
    return total[:, :sources], total[:, sources:]


def solution(mesh):
    n = mesh.shape["row"]

    def body(data_real, data_imag, counts, source_cols):
        rows = data_real.shape[0]
        if rows % 128 == 0 and n == 16:
            return shards(n, data_real, data_imag, counts, source_cols)
        return generic(data_real, data_imag, counts, source_cols)

    placed = (P(("freq", "row"), None), P(("freq", "row"), None), P(), P())
    return jax.shard_map(
        body,
        mesh=mesh,
        in_specs=placed,
        out_specs=(P(("freq", "row"), None), P(("freq", "row"), None)),
        check_vma=False,
    )
```

```python
import functools
import math

import jax
import jax.numpy as jnp
from jax import lax
from jax.experimental import pallas as pl
from jax.experimental.pallas import tpu as pltpu
from jax.sharding import PartitionSpec as P

TILES = 8
NT = (((1,), (1,)), ((), ()))
NN = (((1,), (0,)), ((), ()))


def dot(a, b, dims=NN):
    return lax.dot_general(a, b, dims, preferred_element_type=jnp.float32)


def pick_kernel(info_ref, cols_ref, dr_ref, di_ref, rows_ref, own_ref):
    k = pl.program_id(0)
    height, width = dr_ref.shape
    cols = cols_ref[...]
    sources = cols.shape[0]
    at_row = info_ref[1] + lax.broadcasted_iota(jnp.int32, (sources, height), 1)
    pick_rows = (cols == at_row).astype(jnp.float32).astype(jnp.bfloat16)
    at_col = (2 * k + info_ref[0]) * width + lax.broadcasted_iota(jnp.int32, (sources, width), 1)
    pick_cols = (cols == at_col).astype(jnp.float32).astype(jnp.bfloat16)
    dr = dr_ref[...]
    di = di_ref[...]
    rows_ref[0, :sources, :] = dot(pick_rows, dr).astype(jnp.bfloat16)
    rows_ref[0, sources:, :] = dot(pick_rows, di).astype(jnp.bfloat16)

    @pl.when(k == 0)
    def _():
        own_ref[...] = jnp.zeros_like(own_ref)

    own_ref[:sources, :] += dot(pick_cols, dr, NT)
    own_ref[sources:, :] += dot(pick_cols, di, NT)


def turned(panel):
    half = panel.shape[0] // 2
    return jnp.concatenate([-panel[half:], panel[:half]], axis=0)


def back_kernel(info_ref, scale_ref, panel_ref, dr_ref, di_ref, out_ref):
    j = 2 * pl.program_id(0) + info_ref[0]
    panel = panel_ref[...]
    total = dot(panel, dr_ref[...]) + dot(turned(panel), di_ref[...])
    out_ref[0] = (scale_ref[j] * total).astype(out_ref.dtype)


def front_kernel(scale_ref, panels_ref, dr_ref, di_ref, out_ref):
    j = pl.program_id(0)

    @pl.when(j == 0)
    def _():
        out_ref[...] = jnp.zeros_like(out_ref)

    panel = panels_ref[0]
    out_ref[...] += scale_ref[j] * (dot(dr_ref[...], panel, NT) + dot(di_ref[...], turned(panel), NT))


def final_kernel(front_ref, first_ref, second_ref, real_ref, imag_ref, *, factor):
    sources = first_ref.shape[0]
    real_ref[...] = factor * (front_ref[:, :sources] + first_ref[...].T)
    imag_ref[...] = factor * (front_ref[:, sources:] + second_ref[...].T)


def swap(x, bit):
    n = lax.axis_size("row")
    return lax.ppermute(x, "row", [(i, i ^ (1 << bit)) for i in range(n)])


def halved(x, me, bit, axis):
    mine = (me >> bit) & 1
    got = swap(lax.dynamic_index_in_dim(x, 1 - mine, axis, False).astype(jnp.bfloat16), bit)
    return lax.dynamic_index_in_dim(x, mine, axis, False) + got.astype(x.dtype)


def scattered(kept, got, me):
    half = kept.shape[1] // 2
    total = kept + got.astype(kept.dtype)
    first = total[:, :half].reshape((2, 2, 2) + (half, kept.shape[2]))
    second = total[:, half:].reshape((2, 2, 2) + (half, kept.shape[2]))
    first = halved(first, me, 1, 2)
    second = halved(second, me, 2, 1)
    first = halved(first, me, 2, 1)
    second = halved(second, me, 3, 0)
    first = halved(first, me, 3, 0)
    second = halved(second, me, 1, 0)
    return first, second


def shards(n, data_real, data_imag, counts, source_cols):
    rows, width = data_real.shape
    sources = source_cols.shape[0]
    pair = 2 * sources
    tile = width // TILES
    factor = -1.0 / math.sqrt(width)
    me = lax.axis_index("row")
    core = me & 1
    row0 = me * rows
    table = counts.astype(jnp.float32)
    forward = lax.dynamic_index_in_dim(table, row0 // tile, 0, keepdims=False)
    backward = lax.dynamic_index_in_dim(table, row0 // tile, 1, keepdims=False)
    denom = jnp.maximum(forward + backward, 1.0)
    scale = jnp.repeat(forward / denom, n // TILES)
    smem = pl.BlockSpec(memory_space=pltpu.SMEM)
    params = pltpu.CompilerParams(vmem_limit_bytes=32 << 20)
    large = pltpu.CompilerParams(vmem_limit_bytes=50 << 20)
    cost = pl.CostEstimate(flops=2 * rows * width * pair, bytes_accessed=4 * rows * width, transcendentals=0)
    half_cost = pl.CostEstimate(flops=rows * width * pair, bytes_accessed=2 * rows * width, transcendentals=0)
    whole = lambda shape: pl.BlockSpec(shape, lambda j, *refs: (0,) * len(shape))
    strided = pl.BlockSpec((rows, rows), lambda k, info: (0, 2 * k + info[0]))
    stacked = pl.BlockSpec((1, pair, rows), lambda k, *refs: (k, 0, 0))
    cols = source_cols.reshape(sources, 1)

    def pick(target):
        return pl.pallas_call(
            pick_kernel,
            grid_spec=pltpu.PrefetchScalarGridSpec(
                num_scalar_prefetch=1,
                grid=(n // 2,),
                in_specs=[whole((sources, 1)), strided, strided],
                out_specs=(stacked, whole((pair, rows))),
            ),
            out_shape=(
                jax.ShapeDtypeStruct((n // 2, pair, rows), jnp.bfloat16),
                jax.ShapeDtypeStruct((pair, rows), jnp.float32),
            ),
            compiler_params=large,
            cost_estimate=half_cost,
        )(jnp.stack([target, row0]), cols, data_real, data_imag)

    def back(target, kind, panel):
        return pl.pallas_call(
            back_kernel,
            grid_spec=pltpu.PrefetchScalarGridSpec(
                num_scalar_prefetch=1,
                grid=(n // 2,),
                in_specs=[smem, whole((pair, rows)), strided, strided],
                out_specs=stacked,
            ),
            out_shape=jax.ShapeDtypeStruct((n // 2, pair, rows), kind),
            compiler_params=large,
            cost_estimate=half_cost,
        )(target.reshape(1), scale, panel, data_real, data_imag)

    sent, own_a = pick(1 - core)
    got = swap(sent, 0)
    kept, own_b = pick(core)
    own = own_a + own_b
    tiles = (source_cols // tile)[:, None] == jnp.arange(TILES, dtype=jnp.int32)[None, :]
    w = jnp.tile(jnp.sum(jnp.where(tiles, forward, 0.0), axis=1), 2)[:, None]
    v = jnp.tile(jnp.sum(jnp.where(tiles, backward, 0.0), axis=1), 2)[:, None]
    mirror = jnp.concatenate(scattered(kept, got, me), axis=0).astype(jnp.float32)
    panel = ((w * own + v * mirror) / jnp.maximum(w + v, 1.0)).astype(jnp.bfloat16)
    panels = lax.all_gather(panel, "row", axis=0, tiled=False)
    sent = back(1 - core, jnp.bfloat16, panel)
    got = swap(sent, 0)
    kept = back(core, jnp.float32, panel)
    first, second = scattered(kept, got, me)
    front = pl.pallas_call(
        front_kernel,
        grid=(n,),
        out_shape=jax.ShapeDtypeStruct((rows, pair), jnp.float32),
        in_specs=[
            smem,
            stacked,
            pl.BlockSpec((rows, rows), lambda j: (0, j)),
            pl.BlockSpec((rows, rows), lambda j: (0, j)),
        ],
        out_specs=whole((rows, pair)),
        compiler_params=large,
        cost_estimate=cost,
    )(scale, panels, data_real, data_imag)
    return pl.pallas_call(
        functools.partial(final_kernel, factor=factor),
        out_shape=(jax.ShapeDtypeStruct((rows, sources), jnp.float32),) * 2,
        compiler_params=params,
    )(front, first, second)


def generic(data_real, data_imag, counts, source_cols):
    rows, width = data_real.shape
    sources = source_cols.shape[0]
    tile = width // TILES
    factor = -1.0 / math.sqrt(width)
    row0 = lax.axis_index("row") * rows
    table = counts.astype(jnp.float32)
    forward = lax.dynamic_index_in_dim(table, row0 // tile, 0, keepdims=False)
    backward = lax.dynamic_index_in_dim(table, row0 // tile, 1, keepdims=False)
    scale = jnp.repeat(forward / jnp.maximum(forward + backward, 1.0), tile)
    at_row = row0 + jnp.arange(rows, dtype=jnp.int32)
    pick_rows = (source_cols[:, None] == at_row[None, :]).astype(jnp.bfloat16)
    tn = (((0,), (1,)), ((), ()))
    picked = jnp.concatenate([dot(data_real, pick_rows, tn), dot(data_imag, pick_rows, tn)], axis=1)
    mirror = lax.psum_scatter(picked.astype(jnp.bfloat16), "row", scatter_dimension=0, tiled=True)
    own = jnp.concatenate([jnp.take(data_real, source_cols, axis=1), jnp.take(data_imag, source_cols, axis=1)], axis=1)
    tiles = source_cols // tile
    w = jnp.tile(forward[tiles], 2)[None, :]
    v = jnp.tile(backward[tiles], 2)[None, :]
    panel = (w * own.astype(jnp.float32) + v * mirror.astype(jnp.float32)) / jnp.maximum(w + v, 1.0)
    panel = panel.astype(jnp.bfloat16)
    swap = lambda p: jnp.concatenate([-p[:, sources:], p[:, :sources]], axis=1)
    panels = lax.all_gather(panel, "row", axis=0, tiled=True)
    tt = (((0,), (0,)), ((), ()))
    back = scale[:, None] * (dot(data_real, panel, tt) + dot(data_imag, swap(panel), tt))
    back = lax.psum_scatter(back, "row", scatter_dimension=0, tiled=True)
    steps = jnp.stack([
        s * (
            dot(data_real[:, t * tile : (t + 1) * tile], panels[t * tile : (t + 1) * tile])
            + dot(data_imag[:, t * tile : (t + 1) * tile], swap(panels[t * tile : (t + 1) * tile]))
        )
        for t, s in enumerate(scale[::tile])
    ])
    total = factor * (steps.sum(0) + back)
    return total[:, :sources], total[:, sources:]


def solution(mesh):
    n = mesh.shape["row"]

    def body(data_real, data_imag, counts, source_cols):
        rows = data_real.shape[0]
        if rows % 128 == 0 and n == 16:
            return shards(n, data_real, data_imag, counts, source_cols)
        return generic(data_real, data_imag, counts, source_cols)

    placed = (P(("freq", "row"), None), P(("freq", "row"), None), P(), P())
    return jax.shard_map(
        body,
        mesh=mesh,
        in_specs=placed,
        out_specs=(P(("freq", "row"), None), P(("freq", "row"), None)),
        check_vma=False,
    )
```
